32 devices in a mesh: head: 2 (over y), seq: 16 (over z, x, core).
Axes of the slice: x: 2, y: 2, z: 4, core: 2. Of those that a mesh axis runs over, the one named last changes fastest.
Arguments:
- latent_q: bfloat16 [32, 128, 576], P(None, 'head'), may hold values from -13 to 13
- latent_keys: bfloat16 [16384, 576], P('seq'), may hold values from -10 to 10
- idx_q: bfloat16 [32, 64, 128], replicated, may hold values from -1.5 to 1.5
- idx_keys: bfloat16 [16, 1024, 128], P('seq', 'head'), may hold values from -1.5 to 1.5
- idx_weight: bfloat16 [32, 64], replicated, may hold values from -1.8 to 1.8
Outputs:
- loss: float32 [], replicated
- query_grad: float32 [2048, 128], P(('head', 'seq'))
- weight_grad: float32 [2048], P(('head', 'seq'))
- key_grad: float32 [16, 1024, 128], P('seq', 'head')
The draws below stay inside these ranges and needn't reach their ends.
All inputs are finite; a program needn't handle non-finite values.
Results may differ from the reference program's by a relative error of at most 0.0027.
Values may be sent and summed in bfloat16 or wider, within the bound.
A program may use at most 64 MiB of HBM per device.

```python
import math
import jax
import jax.numpy as jnp
from jax import lax

H = 128
KV_RANK = 512
ROPE = 64
IDX_HEADS = 64
IDX_D = 128
Q = 32
KEY_DEV = 1024
KEYS = 16384
N_SEQ = 16


def draw_everything(key):
    streams = jax.random.split(jax.random.fold_in(key, 7), 6)
    count = KEY_DEV * N_SEQ
    width = KV_RANK + ROPE
    cache = jnp.clip(jax.random.normal(streams[0], (count, width), jnp.float32), -5.0, 5.0)
    row_scale = jnp.exp(jax.random.uniform(streams[1], (count, 1), jnp.float32, math.log(0.5), math.log(2.0)))
    cache = cache * row_scale
    queries = jnp.clip(jax.random.normal(streams[2], (Q, H, width), jnp.float32), -5.0, 5.0)
    index_keys = 0.3 * jnp.clip(jax.random.normal(streams[3], (count, IDX_D), jnp.float32), -5.0, 5.0)
    index_queries = 0.3 * jnp.clip(jax.random.normal(streams[4], (Q, IDX_HEADS, IDX_D), jnp.float32), -5.0, 5.0)
    head_weights = 0.6 * jnp.clip(jax.random.normal(streams[5], (Q, IDX_HEADS), jnp.float32), -3.0, 3.0)
    return (queries, cache, index_queries, index_keys.reshape(N_SEQ, KEY_DEV, IDX_D), head_weights)


def draw_latent_q(key, part):
    return draw_everything(key)[0].astype(jnp.bfloat16)


def draw_latent_keys(key, part):
    return draw_everything(key)[1].astype(jnp.bfloat16)


def draw_idx_q(key, part):
    return draw_everything(key)[2].astype(jnp.bfloat16)


def draw_idx_keys(key, part):
    return draw_everything(key)[3].astype(jnp.bfloat16)


def draw_idx_weight(key, part):
    return draw_everything(key)[4].astype(jnp.bfloat16)


def setup_inputs(seed: int = 0) -> dict:
    arg_keys = jax.random.split(jax.random.key(seed), 6)
    return {
        "latent_q": draw_latent_q(jax.random.fold_in(arg_keys[5], 71), 0),
        "latent_keys": draw_latent_keys(jax.random.fold_in(arg_keys[5], 71), 0),
        "idx_q": draw_idx_q(jax.random.fold_in(arg_keys[5], 71), 0),
        "idx_keys": draw_idx_keys(jax.random.fold_in(arg_keys[5], 71), 0),
        "idx_weight": draw_idx_weight(jax.random.fold_in(arg_keys[5], 71), 0),
    }


softmax_scale = 192 ** -0.5


def plogp(values):
    safe = jnp.where(values > 0, values, 1.0)
    return jnp.where(values > 0, values * jnp.log(safe), 0.0)


def reference(latent_q, latent_keys, idx_q, idx_keys, idx_weight):
    def attend(acc, head_q):
        scores = jnp.dot(head_q, latent_keys.T, preferred_element_type=jnp.float32) * softmax_scale
        top = jnp.max(scores, axis=1, keepdims=True)
        expo = jnp.exp(scores - top)
        return acc + expo / jnp.sum(expo, axis=1, keepdims=True), None

    summed, _ = lax.scan(attend, jnp.zeros((Q, KEYS), jnp.float32), jnp.swapaxes(latent_q, 0, 1))
    targets = summed / H
    keys_flat = idx_keys.reshape(KEYS, IDX_D)
    weights = idx_weight.astype(jnp.float32)
    head_queries = jnp.swapaxes(idx_q, 0, 1)
    head_weights = weights.T

    def score_head(acc, pair):
        head_q, head_w = pair
        act = jnp.dot(head_q, keys_flat.T, preferred_element_type=jnp.float32)
        return acc + head_w[:, None] * jnp.maximum(act, 0.0), None

    logits, _ = lax.scan(score_head, jnp.zeros((Q, KEYS), jnp.float32), (head_queries, head_weights))
    top = jnp.max(logits, axis=1, keepdims=True)
    expo = jnp.exp(logits - top)
    total = jnp.sum(expo, axis=1, keepdims=True)
    loss = jnp.sum(plogp(targets) - targets * (logits - top - jnp.log(total))) / Q
    grad = expo / total - targets

    def back_head(dkeys, pair):
        head_q, head_w = pair
        act = jnp.dot(head_q, keys_flat.T, preferred_element_type=jnp.float32)
        dweight = jnp.sum(grad * jnp.maximum(act, 0.0), axis=1)
        dact = jnp.where(act > 0, grad * head_w[:, None], 0.0).astype(jnp.bfloat16)
        dquery = jnp.dot(dact, keys_flat, preferred_element_type=jnp.float32)
        dkeys = dkeys + jnp.dot(dact.T, head_q, preferred_element_type=jnp.float32)
        return dkeys, (dquery, dweight)

    dkeys, (dquery, dweight) = lax.scan(back_head, jnp.zeros((KEYS, IDX_D), jnp.float32), (head_queries, head_weights))
    return (loss, dquery.reshape(IDX_HEADS * Q, IDX_D), dweight.reshape(IDX_HEADS * Q),
            dkeys.reshape(N_SEQ, KEY_DEV, IDX_D))
```

```python
import functools
import math

import jax
import jax.numpy as jnp
from jax import lax
from jax.experimental import pallas as pl
from jax.experimental.pallas import tpu as pltpu
from jax.sharding import PartitionSpec as P

MESH = pl.DeviceIdType.MESH
NT = (((1,), (1,)), ((), ()))
TN = (((0,), (0,)), ((), ()))
F32 = jnp.float32
BF16 = jnp.bfloat16

exponent_scale = 192 ** (-0.5) * math.log2(math.e)


def to_row(column):
    wide = jnp.broadcast_to(column, (column.shape[0], 128))
    copies = 128 // column.shape[0]
    return jnp.concatenate([wide] * copies, axis=0).T[0:1, :]


def to_column(row, count):
    return jnp.broadcast_to(row, (128, 128)).T[0:count, 0:1]


def join_log2(values):
    top = jnp.max(values, axis=0)
    return top + jnp.log2(jnp.sum(jnp.exp2(values - top[None]), axis=0))


def join_log(values):
    top = jnp.max(values, axis=0)
    return top + jnp.log(jnp.sum(jnp.exp(values - top[None]), axis=0))


def kernel(
    heads_axis, seq_axis, heads, queries_count,
    latent_q, latent_keys, idx_q, keys_ref, weights,
    loss_out, query_out, prod_out, key_out,
    expo, base, stat_all, sum_send, sum_recv, act, dact, term, term_recv, loss_all,
    stat_send_sem, stat_recv_sem, sum_send_sem, sum_recv_sem,
    term_send_sem, term_recv_sem, loss_send_sem, loss_recv_sem,
):
    my_head = lax.axis_index("head")
    my_seq = lax.axis_index("seq")
    devices = heads_axis * seq_axis
    me = my_head * seq_axis + my_seq
    barrier = pltpu.get_barrier_semaphore()

    def place(index):
        return (index // seq_axis, lax.rem(index, seq_axis))

    def greet(offset, carry):
        other = lax.rem(me + offset, devices)
        pl.semaphore_signal(barrier, inc=1, device_id=place(other), device_id_type=MESH)
        return carry

    lax.fori_loop(1, devices, greet, 0)

    rows, width = latent_q.shape
    local_heads = rows // queries_count
    step = 256

    def attend(i, carry):
        columns = pl.ds(pl.multiple_of(i * step, step), step)
        scores = lax.dot_general(
            latent_keys[...], latent_q[columns, :], NT, preferred_element_type=F32
        )
        top = jnp.max(scores, axis=0, keepdims=True)
        part = jnp.exp2((scores - top) * exponent_scale)
        expo[:, columns] = part.astype(BF16)
        total = jnp.sum(part, axis=0, keepdims=True)
        base[:, columns] = top * exponent_scale
        stat_all[my_seq, :, columns] = top * exponent_scale + jnp.log2(total)
        return carry

    lax.fori_loop(0, rows // step, attend, 0)

    blocks, block, _ = weights.shape
    fine = keys_ref.shape[0]
    group = math.gcd(blocks, 8)
    heads_in_block = block // queries_count

    def index_scores(i, logits):
        queries = idx_q[pl.ds(i * group, group)]
        part = lax.dot_general(
            queries.reshape(group * block, -1), keys_ref[...], NT, preferred_element_type=F32
        )
        part = part.reshape(group, block, fine)
        act[pl.ds(i * group, group)] = part
        weighted = weights[pl.ds(i * group, group)] * jnp.maximum(part, 0.0)
        return logits + jnp.sum(
            weighted.reshape(group * heads_in_block, queries_count, fine), axis=0
        )

    logits = lax.fori_loop(
        0, blocks // group, index_scores, jnp.zeros((queries_count, fine), F32)
    )
    index_top = jnp.max(logits, axis=1, keepdims=True)
    index_total = jnp.sum(jnp.exp(logits - index_top), axis=1, keepdims=True)
    stat_all[my_seq, :, rows : rows + 128] = to_row(index_top + jnp.log(index_total))

    pl.semaphore_wait(barrier, devices - 1)

    def stat_copy(offset, source, target):
        return pltpu.make_async_remote_copy(
            src_ref=stat_all.at[source],
            dst_ref=stat_all.at[source],
            send_sem=stat_send_sem.at[offset],
            recv_sem=stat_recv_sem.at[source],
            device_id=(my_head, target),
            device_id_type=MESH,
        )

    def stat_start(offset, carry):
        stat_copy(offset, my_seq, lax.rem(my_seq + offset, seq_axis)).start()
        return carry

    def stat_wait(offset, carry):
        other = lax.rem(my_seq + offset, seq_axis)
        stat_copy(offset, other, other).wait_recv()
        return carry

    def stat_sent(offset, carry):
        stat_copy(offset, my_seq, lax.rem(my_seq + offset, seq_axis)).wait_send()
        return carry

    lax.fori_loop(1, seq_axis, stat_start, 0)
    lax.fori_loop(1, seq_axis, stat_wait, 0)

    joined = join_log2(stat_all[:, :, 0:rows])
    factor = jnp.exp2(base[...] - joined)
    upper = factor.astype(BF16).astype(F32)
    lower = factor - upper
    place_q = lax.broadcasted_iota(jnp.int32, (128, rows), 0)
    start = lax.broadcasted_iota(jnp.int32, (128, rows), 1)
    first = place_q * local_heads
    second = (place_q - queries_count) * local_heads
    in_first = jnp.logical_and(start >= first, start < first + local_heads)
    in_second = jnp.logical_and(start >= second, start < second + local_heads)
    spread = jnp.where(in_first, upper, jnp.where(in_second, lower, 0.0)).astype(BF16)
    summed = lax.dot_general(expo[...], spread, NT, preferred_element_type=F32).T
    summed = summed[0:queries_count] + summed[queries_count : 2 * queries_count]
    index_row = join_log(stat_all[:, :, rows : rows + 128])
    for j in range(heads_axis):
        sum_send[j, 0:queries_count, :] = summed[:, j * fine : (j + 1) * fine]
        sum_send[j, queries_count : queries_count + 1, 0:128] = index_row

    def sum_copy(offset, block_index, slot, target):
        return pltpu.make_async_remote_copy(
            src_ref=sum_send.at[block_index],
            dst_ref=sum_recv.at[slot],
            send_sem=sum_send_sem.at[offset],
            recv_sem=sum_recv_sem.at[slot],
            device_id=(target, my_seq),
            device_id_type=MESH,
        )

    for offset in range(1, heads_axis):
        target = lax.rem(my_head + offset, heads_axis)
        sum_copy(offset, target, my_head, target).start()
    targets = sum_send[my_head, 0:queries_count, :]
    index_rows = [index_row]
    for offset in range(1, heads_axis):
        source = lax.rem(my_head + offset, heads_axis)
        sum_copy(offset, source, source, source).wait_recv()
        targets = targets + sum_recv[source, 0:queries_count, :]
        index_rows.append(sum_recv[source, queries_count : queries_count + 1, 0:128])
    targets = targets / heads
    index_log = to_column(join_log(jnp.stack(index_rows)), queries_count)
    shifted = logits - index_log
    positive = targets > 0
    own_loss = jnp.where(positive, targets * jnp.log(jnp.where(positive, targets, 1.0)), 0.0)
    own_loss = jnp.sum(own_loss - targets * shifted, axis=0, keepdims=True)
    own_loss = sum(own_loss[:, i * 128 : (i + 1) * 128] for i in range(fine // 128))
    grad = jnp.exp(shifted) - targets
    loss_all[me] = own_loss

    def loss_copy(offset, slot, target):
        return pltpu.make_async_remote_copy(
            src_ref=loss_all.at[slot],
            dst_ref=loss_all.at[slot],
            send_sem=loss_send_sem.at[offset],
            recv_sem=loss_recv_sem.at[slot],
            device_id=place(target),
            device_id_type=MESH,
        )

    chunk = term.shape[1]
    owners = block // chunk

    def term_copy(source_slot, slot, target):
        return pltpu.make_async_remote_copy(
            src_ref=term.at[source_slot],
            dst_ref=term_recv.at[slot],
            send_sem=term_send_sem.at[source_slot],
            recv_sem=term_recv_sem.at[slot],
            device_id=place(target),
            device_id_type=MESH,
        )

    grads = jnp.concatenate([grad] * heads_in_block, axis=0)
    grad_upper = grads.astype(BF16).astype(F32)
    grad_lower = grads - grad_upper

    my_block = me // owners

    def back(offset, carry):
        b = lax.rem(my_block + offset, blocks)
        part = act[b]
        on = part > 0
        dact[b] = jnp.where(on, grads * weights[b], 0.0).astype(BF16)
        both = jnp.concatenate(
            [jnp.where(on, grad_upper, 0.0), jnp.where(on, grad_lower, 0.0)], axis=0
        ).astype(BF16)
        result = jnp.dot(both, keys_ref[...], preferred_element_type=F32)
        result = result[0:block] + result[block : 2 * block]
        for j in range(owners):
            owner = b * owners + j
            piece = result[j * chunk : (j + 1) * chunk]
            term[owner] = piece.astype(BF16)

            @pl.when(owner != me)
            def _():
                term_copy(owner, me, owner).start()

        return carry

    lax.fori_loop(1, blocks + 1, back, 0)

    def loss_start(offset, carry):
        loss_copy(offset, me, lax.rem(me + offset, devices)).start()
        return carry

    lax.fori_loop(1, devices, loss_start, 0)

    key_out[...] = lax.dot_general(
        dact[...].reshape(blocks * block, fine),
        idx_q[...].reshape(blocks * block, -1),
        TN,
        preferred_element_type=F32,
    )

    def term_wait(offset, total):
        source = lax.rem(me + offset, devices)
        term_copy(source, source, source).wait_recv()
        return total + term_recv[source].astype(F32)

    total = lax.fori_loop(1, devices, term_wait, term[me].astype(F32))
    own_block = my_block
    inner = me - my_block * owners
    own_weights = weights[own_block]
    own_queries = idx_q[own_block].astype(F32)
    if owners == 1:
        query_out[...] = total * own_weights
        prod_out[...] = total * own_queries
    else:
        for j in range(owners):

            @pl.when(inner == j)
            def _():
                query_out[...] = total * own_weights[j * chunk : (j + 1) * chunk]
                prod_out[...] = total * own_queries[j * chunk : (j + 1) * chunk]

    def loss_wait(offset, carry):
        source = lax.rem(me + offset, devices)
        loss_copy(offset, source, source).wait_recv()
        return carry

    lax.fori_loop(1, devices, loss_wait, 0)
    loss_out[...] = jnp.sum(loss_all[...], axis=0)

    lax.fori_loop(1, seq_axis, stat_sent, 0)
    for offset in range(1, heads_axis):
        target = lax.rem(my_head + offset, heads_axis)
        sum_copy(offset, target, my_head, target).wait_send()

    def last_sent(offset, carry):
        other = lax.rem(me + offset, devices)
        term_copy(other, me, other).wait_send()
        loss_copy(offset, me, other).wait_send()
        return carry

    lax.fori_loop(1, devices, last_sent, 0)


def shards(heads_axis, seq_axis, latent_q, latent_keys, idx_q, idx_keys, idx_weight):
    queries_count, local_heads, width = latent_q.shape
    index_heads, size = idx_q.shape[1:]
    rows = queries_count * local_heads
    keys = latent_keys.shape[0]
    fine = idx_keys.shape[1]
    devices = heads_axis * seq_axis
    all_rows = queries_count * index_heads
    chunk = all_rows // devices
    block = max(chunk, queries_count)
    blocks = all_rows // block
    queries = jnp.swapaxes(idx_q, 0, 1).reshape(blocks, block, size)
    weights = idx_weight.T.astype(F32).reshape(blocks, block, 1)
    vmem = pl.BlockSpec(memory_space=pltpu.VMEM)
    dma = pltpu.SemaphoreType.DMA
    loss, query_grad, prod, key_grad = pl.pallas_call(
        functools.partial(
            kernel, heads_axis, seq_axis, local_heads * heads_axis, queries_count
        ),
        out_shape=(
            jax.ShapeDtypeStruct((1, 128), F32),
            jax.ShapeDtypeStruct((chunk, size), F32),
            jax.ShapeDtypeStruct((chunk, size), F32),
            jax.ShapeDtypeStruct((fine, size), F32),
        ),
        in_specs=[vmem] * 5,
        out_specs=(vmem,) * 4,
        scratch_shapes=[
            pltpu.VMEM((keys, rows), BF16),
            pltpu.VMEM((1, rows), F32),
            pltpu.VMEM((seq_axis, 1, rows + 128), F32),
            pltpu.VMEM((heads_axis, queries_count + 8, fine), F32),
            pltpu.VMEM((heads_axis, queries_count + 8, fine), F32),
            pltpu.VMEM((blocks, block, fine), F32),
            pltpu.VMEM((blocks, block, fine), BF16),
            pltpu.VMEM((devices, chunk, size), BF16),
            pltpu.VMEM((devices, chunk, size), BF16),
            pltpu.VMEM((devices, 1, 128), F32),
            dma((seq_axis,)),
            dma((seq_axis,)),
            dma((heads_axis,)),
            dma((heads_axis,)),
            dma((devices,)),
            dma((devices,)),
            dma((devices,)),
            dma((devices,)),
        ],
        compiler_params=pltpu.CompilerParams(
            collective_id=0, has_side_effects=True, vmem_limit_bytes=60 * 1024 * 1024
        ),
    )(latent_q.reshape(rows, width), latent_keys, queries, idx_keys[0], weights)
    return (
        jnp.sum(loss) / queries_count,
        query_grad,
        jnp.sum(prod, axis=1),
        key_grad[None],
    )


def solution(mesh):
    in_specs = (P(None, "head", None), P("seq", None), P(), P("seq", "head", None), P())
    out_specs = (P(), P(("head", "seq"), None), P(("head", "seq")), P("seq", "head", None))
    body = functools.partial(shards, mesh.shape["head"], mesh.shape["seq"])
    return jax.shard_map(body, mesh=mesh, in_specs=in_specs, out_specs=out_specs, check_vma=False)
```

```python
import functools
import math

import jax
import jax.numpy as jnp
from jax import lax
from jax.experimental import pallas as pl
from jax.experimental.pallas import tpu as pltpu
from jax.sharding import PartitionSpec as P

MESH = pl.DeviceIdType.MESH
NT = (((1,), (1,)), ((), ()))
TN = (((0,), (0,)), ((), ()))
F32 = jnp.float32
BF16 = jnp.bfloat16

exponent_scale = 192 ** (-0.5) * math.log2(math.e)


def to_row(column):
    wide = jnp.broadcast_to(column, (column.shape[0], 128))
    copies = 128 // column.shape[0]
    return jnp.concatenate([wide] * copies, axis=0).T[0:1, :]


def to_column(row, count):
    return jnp.broadcast_to(row, (128, 128)).T[0:count, 0:1]


def join_log2(values):
    top = jnp.max(values, axis=0)
    return top + jnp.log2(jnp.sum(jnp.exp2(values - top[None]), axis=0))


def join_log(values):
    top = jnp.max(values, axis=0)
    return top + jnp.log(jnp.sum(jnp.exp(values - top[None]), axis=0))


def kernel(
    heads_axis, seq_axis, heads, queries_count,
    latent_q, latent_keys, idx_q, keys_ref, weight_ref,
    loss_out, query_out, prod_out, key_out,
    weights, own_term, pair_recv, expo, base, stat_all, sum_send, sum_recv, act, dact, term, term_recv, loss_all,
    stat_send_sem, stat_recv_sem, sum_send_sem, sum_recv_sem,
    term_send_sem, term_recv_sem, loss_send_sem, loss_recv_sem, pair_send_sem, pair_recv_sem,
):
    my_head = lax.axis_index("head")
    my_seq = lax.axis_index("seq")
    devices = heads_axis * seq_axis
    me = my_head * seq_axis + my_seq
    barrier = pltpu.get_barrier_semaphore()

    def place(index):
        return (index // seq_axis, lax.rem(index, seq_axis))

    def greet(offset, carry):
        other = lax.rem(me + offset, devices)
        pl.semaphore_signal(barrier, inc=1, device_id=place(other), device_id_type=MESH)
        return carry

    lax.fori_loop(1, devices, greet, 0)

    rows, width = latent_q.shape
    local_heads = rows // queries_count
    step = 256

    def attend(i, carry):
        columns = pl.ds(pl.multiple_of(i * step, step), step)
        scores = lax.dot_general(
            latent_keys[...], latent_q[columns, :], NT, preferred_element_type=F32
        )
        top = jnp.max(scores, axis=0, keepdims=True)
        part = jnp.exp2((scores - top) * exponent_scale)
        expo[:, columns] = part.astype(BF16)
        total = jnp.sum(part, axis=0, keepdims=True)
        base[:, columns] = top * exponent_scale
        stat_all[my_seq, :, columns] = top * exponent_scale + jnp.log2(total)
        return carry

    lax.fori_loop(0, rows // step, attend, 0)

    blocks, block, _ = weights.shape
    fine = keys_ref.shape[0]
    group = math.gcd(blocks, 8)
    heads_in_block = block // queries_count
    wide = weight_ref[...].astype(F32)
    for g in range(wide.shape[1]):
        row = g % heads_in_block * queries_count
        weights[g // heads_in_block, row : row + queries_count, :] = wide[:, g : g + 1]

    def index_scores(i, logits):
        queries = idx_q[pl.ds(i * group, group)]
        part = lax.dot_general(
            queries.reshape(group * block, -1), keys_ref[...], NT, preferred_element_type=F32
        )
        part = part.reshape(group, block, fine)
        act[pl.ds(i * group, group)] = part
        weighted = weights[pl.ds(i * group, group)] * jnp.maximum(part, 0.0)
        return logits + jnp.sum(
            weighted.reshape(group * heads_in_block, queries_count, fine), axis=0
        )

    logits = lax.fori_loop(
        0, blocks // group, index_scores, jnp.zeros((queries_count, fine), F32)
    )
    index_top = jnp.max(logits, axis=1, keepdims=True)
    index_total = jnp.sum(jnp.exp(logits - index_top), axis=1, keepdims=True)
    stat_all[my_seq, :, rows : rows + 128] = to_row(index_top + jnp.log(index_total))

    pl.semaphore_wait(barrier, devices - 1)

    def stat_copy(offset, source, target):
        return pltpu.make_async_remote_copy(
            src_ref=stat_all.at[source],
            dst_ref=stat_all.at[source],
            send_sem=stat_send_sem.at[offset],
            recv_sem=stat_recv_sem.at[source],
            device_id=(my_head, target),
            device_id_type=MESH,
        )

    def stat_start(offset, carry):
        stat_copy(offset, my_seq, lax.rem(my_seq + offset, seq_axis)).start()
        return carry

    def stat_wait(offset, carry):
        other = lax.rem(my_seq + offset, seq_axis)
        stat_copy(offset, other, other).wait_recv()
        return carry

    def stat_sent(offset, carry):
        stat_copy(offset, my_seq, lax.rem(my_seq + offset, seq_axis)).wait_send()
        return carry

    lax.fori_loop(1, seq_axis, stat_start, 0)
    lax.fori_loop(1, seq_axis, stat_wait, 0)

    joined = join_log2(stat_all[:, :, 0:rows])
    factor = jnp.exp2(base[...] - joined)
    upper = factor.astype(BF16).astype(F32)
    lower = factor - upper
    place_q = lax.broadcasted_iota(jnp.int32, (128, rows), 0)
    start = lax.broadcasted_iota(jnp.int32, (128, rows), 1)
    first = place_q * local_heads
    second = (place_q - queries_count) * local_heads
    in_first = jnp.logical_and(start >= first, start < first + local_heads)
    in_second = jnp.logical_and(start >= second, start < second + local_heads)
    spread = jnp.where(in_first, upper, jnp.where(in_second, lower, 0.0)).astype(BF16)
    summed = lax.dot_general(expo[...], spread, NT, preferred_element_type=F32).T
    summed = summed[0:queries_count] + summed[queries_count : 2 * queries_count]
    index_row = join_log(stat_all[:, :, rows : rows + 128])
    for j in range(heads_axis):
        sum_send[j, 0:queries_count, :] = summed[:, j * fine : (j + 1) * fine]
        sum_send[j, queries_count : queries_count + 1, 0:128] = index_row

    def sum_copy(offset, block_index, slot, target):
        return pltpu.make_async_remote_copy(
            src_ref=sum_send.at[block_index],
            dst_ref=sum_recv.at[slot],
            send_sem=sum_send_sem.at[offset],
            recv_sem=sum_recv_sem.at[slot],
            device_id=(target, my_seq),
            device_id_type=MESH,
        )

    for offset in range(1, heads_axis):
        target = lax.rem(my_head + offset, heads_axis)
        sum_copy(offset, target, my_head, target).start()
    targets = sum_send[my_head, 0:queries_count, :]
    index_rows = [index_row]
    for offset in range(1, heads_axis):
        source = lax.rem(my_head + offset, heads_axis)
        sum_copy(offset, source, source, source).wait_recv()
        targets = targets + sum_recv[source, 0:queries_count, :]
        index_rows.append(sum_recv[source, queries_count : queries_count + 1, 0:128])
    targets = targets / heads
    index_log = to_column(join_log(jnp.stack(index_rows)), queries_count)
    shifted = logits - index_log
    positive = targets > 0
    own_loss = jnp.where(positive, targets * jnp.log(jnp.where(positive, targets, 1.0)), 0.0)
    own_loss = jnp.sum(own_loss - targets * shifted, axis=0, keepdims=True)
    own_loss = sum(own_loss[:, i * 128 : (i + 1) * 128] for i in range(fine // 128))
    grad = jnp.exp(shifted) - targets
    loss_all[me] = own_loss

    def loss_copy(offset, slot, target):
        return pltpu.make_async_remote_copy(
            src_ref=loss_all.at[slot],
            dst_ref=loss_all.at[slot],
            send_sem=loss_send_sem.at[offset],
            recv_sem=loss_recv_sem.at[slot],
            device_id=place(target),
            device_id_type=MESH,
        )

    chunk = term.shape[1]
    owners = block // chunk

    def term_copy(source_slot, slot, target):
        return pltpu.make_async_remote_copy(
            src_ref=term.at[source_slot],
            dst_ref=term_recv.at[slot],
            send_sem=term_send_sem.at[source_slot],
            recv_sem=term_recv_sem.at[slot],
            device_id=place(target),
            device_id_type=MESH,
        )

    grads = jnp.concatenate([grad] * heads_in_block, axis=0)
    grad_upper = grads.astype(BF16).astype(F32)
    grad_lower = grads - grad_upper

    my_block = me // owners
    parity = lax.rem(my_seq, 2)
    pair = my_seq + 1 - 2 * parity

    def pair_copy(owner):
        return pltpu.make_async_remote_copy(
            src_ref=own_term.at[owner],
            dst_ref=pair_recv.at[owner],
            send_sem=pair_send_sem.at[owner],
            recv_sem=pair_recv_sem.at[owner],
            device_id=(my_head, pair),
            device_id_type=MESH,
        )

    def back(b):
        part = act[b]
        on = part > 0
        dact[b] = jnp.where(on, grads * weights[b], 0.0).astype(BF16)
        both = jnp.concatenate(
            [jnp.where(on, grad_upper, 0.0), jnp.where(on, grad_lower, 0.0)], axis=0
        ).astype(BF16)
        result = jnp.dot(both, keys_ref[...], preferred_element_type=F32)
        result = result[0:block] + result[block : 2 * block]
        for j in range(owners):
            own_term[b * owners + j] = result[j * chunk : (j + 1) * chunk]

    def finish(owner):
        pair_copy(owner).wait_recv()
        term[owner] = (own_term[owner] + pair_recv[owner]).astype(BF16)

        @pl.when(owner != me)
        def _():
            term_copy(owner, me, owner).start()

    half = devices // 2

    def partner_owner(offset):
        return lax.rem(2 * (me // 2 + offset), devices) + 1 - parity

    def kept_owner(offset):
        return lax.rem(2 * (me // 2 + offset), devices) + parity

    if owners == 1:

        def first_half(offset, carry):
            back(partner_owner(offset))
            pair_copy(partner_owner(offset)).start()
            return carry

        def second_half(offset, carry):
            back(kept_owner(offset))
            finish(kept_owner(offset))
            return carry

        lax.fori_loop(1, half + 1, first_half, 0)
        lax.fori_loop(1, half + 1, second_half, 0)
    else:

        def every_block(b, carry):
            back(b)
            return carry

        def pair_start(offset, carry):
            pair_copy(partner_owner(offset)).start()
            return carry

        def finish_all(offset, carry):
            finish(kept_owner(offset))
            return carry

        lax.fori_loop(0, blocks, every_block, 0)
        lax.fori_loop(1, half + 1, pair_start, 0)
        lax.fori_loop(1, half + 1, finish_all, 0)

    def loss_start(offset, carry):
        loss_copy(offset, me, lax.rem(me + offset, devices)).start()
        return carry

    lax.fori_loop(1, devices, loss_start, 0)

    key_out[...] = lax.dot_general(
        dact[...].reshape(blocks * block, fine),
        idx_q[...].reshape(blocks * block, -1),
        TN,
        preferred_element_type=F32,
    )

    def term_wait(offset, total):
        source = kept_owner(offset)
        term_copy(source, source, source).wait_recv()
        return total + term_recv[source].astype(F32)

    total = lax.fori_loop(1, half, term_wait, own_term[me] + pair_recv[me])
    own_block = my_block
    inner = me - my_block * owners
    own_weights = weights[own_block]
    own_queries = idx_q[own_block].astype(F32)
    if owners == 1:
        query_out[...] = total * own_weights
        prod_out[...] = total * own_queries
    else:
        for j in range(owners):

            @pl.when(inner == j)
            def _():
                query_out[...] = total * own_weights[j * chunk : (j + 1) * chunk]
                prod_out[...] = total * own_queries[j * chunk : (j + 1) * chunk]

    def loss_wait(offset, carry):
        source = lax.rem(me + offset, devices)
        loss_copy(offset, source, source).wait_recv()
        return carry

    lax.fori_loop(1, devices, loss_wait, 0)
    loss_out[...] = jnp.sum(loss_all[...], axis=0)

    lax.fori_loop(1, seq_axis, stat_sent, 0)
    for offset in range(1, heads_axis):
        target = lax.rem(my_head + offset, heads_axis)
        sum_copy(offset, target, my_head, target).wait_send()

    def last_sent(offset, carry):
        other = lax.rem(me + offset, devices)
        loss_copy(offset, me, other).wait_send()
        return carry

    def half_sent(offset, carry):
        term_copy(kept_owner(offset), me, kept_owner(offset)).wait_send()
        return carry

    def pair_sent(offset, carry):
        pair_copy(partner_owner(offset)).wait_send()
        return carry

    lax.fori_loop(1, devices, last_sent, 0)
    lax.fori_loop(1, half, half_sent, 0)
    lax.fori_loop(1, half + 1, pair_sent, 0)


def closing(queries_count, loss_in, query_in, prod_in, key_in, loss_out, query_out, weight_out, key_out):
    loss_out[...] = jnp.sum(loss_in[...], axis=1, keepdims=True) / queries_count
    query_out[...] = query_in[...]
    ones = jnp.ones((8, prod_in.shape[1]), F32)
    sums = lax.dot_general(
        ones, prod_in[...], NT, precision=lax.Precision.HIGHEST, preferred_element_type=F32
    )
    weight_out[...] = sums[0:1]
    key_out[...] = key_in[...]


def shards(heads_axis, seq_axis, latent_q, latent_keys, idx_q, idx_keys, idx_weight):
    queries_count, local_heads, width = latent_q.shape
    index_heads, size = idx_q.shape[1:]
    rows = queries_count * local_heads
    keys = latent_keys.shape[0]
    fine = idx_keys.shape[1]
    devices = heads_axis * seq_axis
    all_rows = queries_count * index_heads
    chunk = all_rows // devices
    block = max(chunk, queries_count)
    blocks = all_rows // block
    queries = jnp.swapaxes(idx_q, 0, 1).reshape(blocks, block, size)
    vmem = pl.BlockSpec(memory_space=pltpu.VMEM)
    dma = pltpu.SemaphoreType.DMA
    loss, query_grad, prod, key_grad = pl.pallas_call(
        functools.partial(
            kernel, heads_axis, seq_axis, local_heads * heads_axis, queries_count
        ),
        out_shape=(
            jax.ShapeDtypeStruct((1, 128), F32),
            jax.ShapeDtypeStruct((chunk, size), F32),
            jax.ShapeDtypeStruct((chunk, size), F32),
            jax.ShapeDtypeStruct((fine, size), F32),
        ),
        in_specs=[vmem] * 5,
        out_specs=(vmem,) * 4,
        scratch_shapes=[
            pltpu.VMEM((blocks, block, 1), F32),
            pltpu.VMEM((devices, chunk, size), F32),
            pltpu.VMEM((devices, chunk, size), F32),
            pltpu.VMEM((keys, rows), BF16),
            pltpu.VMEM((1, rows), F32),
            pltpu.VMEM((seq_axis, 1, rows + 128), F32),
            pltpu.VMEM((heads_axis, queries_count + 8, fine), F32),
            pltpu.VMEM((heads_axis, queries_count + 8, fine), F32),
            pltpu.VMEM((blocks, block, fine), F32),
            pltpu.VMEM((blocks, block, fine), BF16),
            pltpu.VMEM((devices, chunk, size), BF16),
            pltpu.VMEM((devices, chunk, size), BF16),
            pltpu.VMEM((devices, 1, 128), F32),
            dma((seq_axis,)),
            dma((seq_axis,)),
            dma((heads_axis,)),
            dma((heads_axis,)),
            dma((devices,)),
            dma((devices,)),
            dma((devices,)),
            dma((devices,)),
            dma((devices,)),
            dma((devices,)),
        ],
        compiler_params=pltpu.CompilerParams(
            collective_id=0, has_side_effects=True, vmem_limit_bytes=60 * 1024 * 1024
        ),
    )(latent_q.reshape(rows, width), latent_keys, queries, idx_keys[0], idx_weight)
    loss, query_grad, weight_grad, key_grad = pl.pallas_call(
        functools.partial(closing, queries_count),
        out_shape=(
            jax.ShapeDtypeStruct((1, 1), F32),
            jax.ShapeDtypeStruct((chunk, size), F32),
            jax.ShapeDtypeStruct((1, chunk), F32),
            jax.ShapeDtypeStruct((fine, size), F32),
        ),
        in_specs=[vmem] * 4,
        out_specs=(vmem,) * 4,
    )(loss, query_grad, prod, key_grad)
    return (loss.reshape(()), query_grad, weight_grad.reshape(-1), key_grad[None])


def solution(mesh):
    in_specs = (P(None, "head", None), P("seq", None), P(), P("seq", "head", None), P())
    out_specs = (P(), P(("head", "seq"), None), P(("head", "seq")), P("seq", "head", None))
    body = functools.partial(shards, mesh.shape["head"], mesh.shape["seq"])
    return jax.shard_map(body, mesh=mesh, in_specs=in_specs, out_specs=out_specs, check_vma=False)
```

```python
import functools
import math

import jax
import jax.numpy as jnp
from jax import lax
from jax.experimental import pallas as pl
from jax.experimental.pallas import tpu as pltpu
from jax.sharding import PartitionSpec as P

MESH = pl.DeviceIdType.MESH
NT = (((1,), (1,)), ((), ()))
TN = (((0,), (0,)), ((), ()))
F32 = jnp.float32
BF16 = jnp.bfloat16

exponent_scale = 192 ** (-0.5) * math.log2(math.e)


def to_row(column):
    wide = jnp.broadcast_to(column, (column.shape[0], 128))
    copies = 128 // column.shape[0]
    return jnp.concatenate([wide] * copies, axis=0).T[0:1, :]


def to_column(row, count):
    return jnp.broadcast_to(row, (128, 128)).T[0:count, 0:1]


def join_log2(values):
    top = jnp.max(values, axis=0)
    return top + jnp.log2(jnp.sum(jnp.exp2(values - top[None]), axis=0))


def join_log(values):
    top = jnp.max(values, axis=0)
    return top + jnp.log(jnp.sum(jnp.exp(values - top[None]), axis=0))


def kernel(
    heads_axis, seq_axis, heads, queries_count,
    latent_q, turned_keys, query_ref, keys_ref, weight_ref,
    loss_out, query_out, prod_out, key_out,
    latent_keys, idx_q, flat_queries, weights, own_term, pair_recv, expo, base, stat_all, sum_send, sum_recv, act, dact, term, term_recv, loss_all,
    stat_send_sem, stat_recv_sem, sum_send_sem, sum_recv_sem,
    term_send_sem, term_recv_sem, loss_send_sem, loss_recv_sem, pair_send_sem, pair_recv_sem,
):
    my_head = lax.axis_index("head")
    my_seq = lax.axis_index("seq")
    devices = heads_axis * seq_axis
    me = my_head * seq_axis + my_seq
    barrier = pltpu.get_barrier_semaphore()

    def place(index):
        return (index // seq_axis, lax.rem(index, seq_axis))

    def greet(offset, carry):
        other = lax.rem(me + offset, devices)
        pl.semaphore_signal(barrier, inc=1, device_id=place(other), device_id_type=MESH)
        return carry

    lax.fori_loop(1, devices, greet, 0)

    rows, width = latent_q.shape
    local_heads = rows // queries_count
    step = 256
    latent_keys[...] = turned_keys[...].T

    def attend(i, carry):
        columns = pl.ds(pl.multiple_of(i * step, step), step)
        scores = lax.dot_general(
            latent_keys[...], latent_q[columns, :], NT, preferred_element_type=F32
        )
        top = jnp.max(scores, axis=0, keepdims=True)
        part = jnp.exp2((scores - top) * exponent_scale)
        expo[:, columns] = part.astype(BF16)
        total = jnp.sum(part, axis=0, keepdims=True)
        base[:, columns] = top * exponent_scale
        stat_all[my_seq, :, columns] = top * exponent_scale + jnp.log2(total)
        return carry

    lax.fori_loop(0, rows // step, attend, 0)

    blocks, block, _ = weights.shape
    fine = keys_ref.shape[0]
    group = math.gcd(blocks, 8)
    heads_in_block = block // queries_count
    wide = weight_ref[...].astype(F32)
    flat_queries[...] = query_ref[...].astype(F32)
    index_heads = wide.shape[1]
    for g in range(wide.shape[1]):
        row = g % heads_in_block * queries_count
        weights[g // heads_in_block, row : row + queries_count, :] = wide[:, g : g + 1]
        picked = flat_queries[pl.ds(g, queries_count, stride=index_heads), :]
        idx_q[g // heads_in_block, row : row + queries_count, :] = picked.astype(BF16)

    def index_scores(i, logits):
        queries = idx_q[pl.ds(i * group, group)]
        part = lax.dot_general(
            queries.reshape(group * block, -1), keys_ref[...], NT, preferred_element_type=F32
        )
        part = part.reshape(group, block, fine)
        act[pl.ds(i * group, group)] = part
        weighted = weights[pl.ds(i * group, group)] * jnp.maximum(part, 0.0)
        return logits + jnp.sum(
            weighted.reshape(group * heads_in_block, queries_count, fine), axis=0
        )

    logits = lax.fori_loop(
        0, blocks // group, index_scores, jnp.zeros((queries_count, fine), F32)
    )
    index_top = jnp.max(logits, axis=1, keepdims=True)
    index_total = jnp.sum(jnp.exp(logits - index_top), axis=1, keepdims=True)
    stat_all[my_seq, :, rows : rows + 128] = to_row(index_top + jnp.log(index_total))

    pl.semaphore_wait(barrier, devices - 1)

    def stat_copy(offset, source, target):
        return pltpu.make_async_remote_copy(
            src_ref=stat_all.at[source],
            dst_ref=stat_all.at[source],
            send_sem=stat_send_sem.at[offset],
            recv_sem=stat_recv_sem.at[source],
            device_id=(my_head, target),
            device_id_type=MESH,
        )

    def stat_start(offset, carry):
        stat_copy(offset, my_seq, lax.rem(my_seq + offset, seq_axis)).start()
        return carry

    def stat_wait(offset, carry):
        other = lax.rem(my_seq + offset, seq_axis)
        stat_copy(offset, other, other).wait_recv()
        return carry

    def stat_sent(offset, carry):
        stat_copy(offset, my_seq, lax.rem(my_seq + offset, seq_axis)).wait_send()
        return carry

    lax.fori_loop(1, seq_axis, stat_start, 0)
    lax.fori_loop(1, seq_axis, stat_wait, 0)

    joined = join_log2(stat_all[:, :, 0:rows])
    factor = jnp.exp2(base[...] - joined)
    upper = factor.astype(BF16).astype(F32)
    lower = factor - upper
    place_q = lax.broadcasted_iota(jnp.int32, (128, rows), 0)
    start = lax.broadcasted_iota(jnp.int32, (128, rows), 1)
    first = place_q * local_heads
    second = (place_q - queries_count) * local_heads
    in_first = jnp.logical_and(start >= first, start < first + local_heads)
    in_second = jnp.logical_and(start >= second, start < second + local_heads)
    spread = jnp.where(in_first, upper, jnp.where(in_second, lower, 0.0)).astype(BF16)
    summed = lax.dot_general(expo[...], spread, NT, preferred_element_type=F32).T
    summed = summed[0:queries_count] + summed[queries_count : 2 * queries_count]
    index_row = join_log(stat_all[:, :, rows : rows + 128])
    for j in range(heads_axis):
        sum_send[j, 0:queries_count, :] = summed[:, j * fine : (j + 1) * fine]
        sum_send[j, queries_count : queries_count + 1, 0:128] = index_row

    def sum_copy(offset, block_index, slot, target):
        return pltpu.make_async_remote_copy(
            src_ref=sum_send.at[block_index],
            dst_ref=sum_recv.at[slot],
            send_sem=sum_send_sem.at[offset],
            recv_sem=sum_recv_sem.at[slot],
            device_id=(target, my_seq),
            device_id_type=MESH,
        )

    for offset in range(1, heads_axis):
        target = lax.rem(my_head + offset, heads_axis)
        sum_copy(offset, target, my_head, target).start()
    targets = sum_send[my_head, 0:queries_count, :]
    index_rows = [index_row]
    for offset in range(1, heads_axis):
        source = lax.rem(my_head + offset, heads_axis)
        sum_copy(offset, source, source, source).wait_recv()
        targets = targets + sum_recv[source, 0:queries_count, :]
        index_rows.append(sum_recv[source, queries_count : queries_count + 1, 0:128])
    targets = targets / heads
    index_log = to_column(join_log(jnp.stack(index_rows)), queries_count)
    shifted = logits - index_log
    positive = targets > 0
    own_loss = jnp.where(positive, targets * jnp.log(jnp.where(positive, targets, 1.0)), 0.0)
    own_loss = jnp.sum(own_loss - targets * shifted, axis=0, keepdims=True)
    own_loss = sum(own_loss[:, i * 128 : (i + 1) * 128] for i in range(fine // 128))
    grad = jnp.exp(shifted) - targets
    loss_all[me] = own_loss

    def loss_copy(offset, slot, target):
        return pltpu.make_async_remote_copy(
            src_ref=loss_all.at[slot],
            dst_ref=loss_all.at[slot],
            send_sem=loss_send_sem.at[offset],
            recv_sem=loss_recv_sem.at[slot],
            device_id=place(target),
            device_id_type=MESH,
        )

    chunk = term.shape[1]
    owners = block // chunk

    def term_copy(source_slot, slot, target):
        return pltpu.make_async_remote_copy(
            src_ref=term.at[source_slot],
            dst_ref=term_recv.at[slot],
            send_sem=term_send_sem.at[source_slot],
            recv_sem=term_recv_sem.at[slot],
            device_id=place(target),
            device_id_type=MESH,
        )

    grads = jnp.concatenate([grad] * heads_in_block, axis=0)
    grad_upper = grads.astype(BF16).astype(F32)
    grad_lower = grads - grad_upper

    my_block = me // owners
    parity = lax.rem(my_seq, 2)
    pair = my_seq + 1 - 2 * parity

    def pair_copy(owner):
        return pltpu.make_async_remote_copy(
            src_ref=own_term.at[owner],
            dst_ref=pair_recv.at[owner],
            send_sem=pair_send_sem.at[owner],
            recv_sem=pair_recv_sem.at[owner],
            device_id=(my_head, pair),
            device_id_type=MESH,
        )

    def back(b):
        part = act[b]
        on = part > 0
        dact[b] = jnp.where(on, grads * weights[b], 0.0).astype(BF16)
        both = jnp.concatenate(
            [jnp.where(on, grad_upper, 0.0), jnp.where(on, grad_lower, 0.0)], axis=0
        ).astype(BF16)
        result = jnp.dot(both, keys_ref[...], preferred_element_type=F32)
        result = result[0:block] + result[block : 2 * block]
        for j in range(owners):
            own_term[b * owners + j] = result[j * chunk : (j + 1) * chunk]

    def finish(owner):
        pair_copy(owner).wait_recv()
        term[owner] = (own_term[owner] + pair_recv[owner]).astype(BF16)

        @pl.when(owner != me)
        def _():
            term_copy(owner, me, owner).start()

    half = devices // 2

    def partner_owner(offset):
        return lax.rem(2 * (me // 2 + offset), devices) + 1 - parity

    def kept_owner(offset):
        return lax.rem(2 * (me // 2 + offset), devices) + parity

    if owners == 1:

        def first_half(offset, carry):
            back(partner_owner(offset))
            pair_copy(partner_owner(offset)).start()
            return carry

        def second_half(offset, carry):
            back(kept_owner(offset))
            finish(kept_owner(offset))
            return carry

        lax.fori_loop(1, half + 1, first_half, 0)
        lax.fori_loop(1, half + 1, second_half, 0)
    else:

        def every_block(b, carry):
            back(b)
            return carry

        def pair_start(offset, carry):
            pair_copy(partner_owner(offset)).start()
            return carry

        def finish_all(offset, carry):
            finish(kept_owner(offset))
            return carry

        lax.fori_loop(0, blocks, every_block, 0)
        lax.fori_loop(1, half + 1, pair_start, 0)
        lax.fori_loop(1, half + 1, finish_all, 0)

    def loss_start(offset, carry):
        loss_copy(offset, me, lax.rem(me + offset, devices)).start()
        return carry

    lax.fori_loop(1, devices, loss_start, 0)

    key_out[...] = lax.dot_general(
        dact[...].reshape(blocks * block, fine),
        idx_q[...].reshape(blocks * block, -1),
        TN,
        preferred_element_type=F32,
    )

    def term_wait(offset, total):
        source = kept_owner(offset)
        term_copy(source, source, source).wait_recv()
        return total + term_recv[source].astype(F32)

    total = lax.fori_loop(1, half, term_wait, own_term[me] + pair_recv[me])
    own_block = my_block
    inner = me - my_block * owners
    own_weights = weights[own_block]
    own_queries = idx_q[own_block].astype(F32)
    if owners == 1:
        query_out[...] = total * own_weights
        prod_out[...] = total * own_queries
    else:
        for j in range(owners):

            @pl.when(inner == j)
            def _():
                query_out[...] = total * own_weights[j * chunk : (j + 1) * chunk]
                prod_out[...] = total * own_queries[j * chunk : (j + 1) * chunk]

    def loss_wait(offset, carry):
        source = lax.rem(me + offset, devices)
        loss_copy(offset, source, source).wait_recv()
        return carry

    lax.fori_loop(1, devices, loss_wait, 0)
    loss_out[...] = jnp.sum(loss_all[...], axis=0)

    lax.fori_loop(1, seq_axis, stat_sent, 0)
    for offset in range(1, heads_axis):
        target = lax.rem(my_head + offset, heads_axis)
        sum_copy(offset, target, my_head, target).wait_send()

    def last_sent(offset, carry):
        other = lax.rem(me + offset, devices)
        loss_copy(offset, me, other).wait_send()
        return carry

    def half_sent(offset, carry):
        term_copy(kept_owner(offset), me, kept_owner(offset)).wait_send()
        return carry

    def pair_sent(offset, carry):
        pair_copy(partner_owner(offset)).wait_send()
        return carry

    lax.fori_loop(1, devices, last_sent, 0)
    lax.fori_loop(1, half, half_sent, 0)
    lax.fori_loop(1, half + 1, pair_sent, 0)


def closing(queries_count, loss_in, query_in, prod_in, key_in, loss_out, query_out, weight_out, key_out):
    loss_out[...] = jnp.sum(loss_in[...], axis=1, keepdims=True) / queries_count
    query_out[...] = query_in[...]
    ones = jnp.ones((8, prod_in.shape[1]), F32)
    sums = lax.dot_general(
        ones, prod_in[...], NT, precision=lax.Precision.HIGHEST, preferred_element_type=F32
    )
    weight_out[...] = sums[0:1]
    key_out[...] = key_in[...]


def shards(heads_axis, seq_axis, latent_q, latent_keys, idx_q, idx_keys, idx_weight):
    queries_count, local_heads, width = latent_q.shape
    index_heads, size = idx_q.shape[1:]
    rows = queries_count * local_heads
    keys = latent_keys.shape[0]
    fine = idx_keys.shape[1]
    devices = heads_axis * seq_axis
    all_rows = queries_count * index_heads
    chunk = all_rows // devices
    block = max(chunk, queries_count)
    blocks = all_rows // block
    queries = idx_q.reshape(all_rows, size)
    vmem = pl.BlockSpec(memory_space=pltpu.VMEM)
    dma = pltpu.SemaphoreType.DMA
    loss, query_grad, prod, key_grad = pl.pallas_call(
        functools.partial(
            kernel, heads_axis, seq_axis, local_heads * heads_axis, queries_count
        ),
        out_shape=(
            jax.ShapeDtypeStruct((1, 128), F32),
            jax.ShapeDtypeStruct((chunk, size), F32),
            jax.ShapeDtypeStruct((chunk, size), F32),
            jax.ShapeDtypeStruct((fine, size), F32),
        ),
        in_specs=[vmem] * 5,
        out_specs=(vmem,) * 4,
        scratch_shapes=[
            pltpu.VMEM((keys, width), BF16),
            pltpu.VMEM((blocks, block, size), BF16),
            pltpu.VMEM((all_rows, size), F32),
            pltpu.VMEM((blocks, block, 1), F32),
            pltpu.VMEM((devices, chunk, size), F32),
            pltpu.VMEM((devices, chunk, size), F32),
            pltpu.VMEM((keys, rows), BF16),
            pltpu.VMEM((1, rows), F32),
            pltpu.VMEM((seq_axis, 1, rows + 128), F32),
            pltpu.VMEM((heads_axis, queries_count + 8, fine), F32),
            pltpu.VMEM((heads_axis, queries_count + 8, fine), F32),
            pltpu.VMEM((blocks, block, fine), F32),
            pltpu.VMEM((blocks, block, fine), BF16),
            pltpu.VMEM((devices, chunk, size), BF16),
            pltpu.VMEM((devices, chunk, size), BF16),
            pltpu.VMEM((devices, 1, 128), F32),
            dma((seq_axis,)),
            dma((seq_axis,)),
            dma((heads_axis,)),
            dma((heads_axis,)),
            dma((devices,)),
            dma((devices,)),
            dma((devices,)),
            dma((devices,)),
            dma((devices,)),
            dma((devices,)),
        ],
        compiler_params=pltpu.CompilerParams(
            collective_id=0, has_side_effects=True, vmem_limit_bytes=60 * 1024 * 1024
        ),
    )(latent_q.reshape(rows, width), latent_keys.T, queries, idx_keys[0], idx_weight)
    loss, query_grad, weight_grad, key_grad = pl.pallas_call(
        functools.partial(closing, queries_count),
        out_shape=(
            jax.ShapeDtypeStruct((1, 1), F32),
            jax.ShapeDtypeStruct((chunk, size), F32),
            jax.ShapeDtypeStruct((1, chunk), F32),
            jax.ShapeDtypeStruct((fine, size), F32),
        ),
        in_specs=[vmem] * 4,
        out_specs=(vmem,) * 4,
    )(loss, query_grad, prod, key_grad)
    return (loss.reshape(()), query_grad, weight_grad.reshape(-1), key_grad[None])


def solution(mesh):
    in_specs = (P(None, "head", None), P("seq", None), P(), P("seq", "head", None), P())
    out_specs = (P(), P(("head", "seq"), None), P(("head", "seq")), P("seq", "head", None))
    body = functools.partial(shards, mesh.shape["head"], mesh.shape["seq"])
    return jax.shard_map(body, mesh=mesh, in_specs=in_specs, out_specs=out_specs, check_vma=False)
```

```python
import functools
import math

import jax
import jax.numpy as jnp
from jax import lax
from jax.experimental import pallas as pl
from jax.experimental.pallas import tpu as pltpu
from jax.sharding import PartitionSpec as P

MESH = pl.DeviceIdType.MESH
NT = (((1,), (1,)), ((), ()))
TN = (((0,), (0,)), ((), ()))
F32 = jnp.float32
BF16 = jnp.bfloat16

exponent_scale = 192 ** (-0.5) * math.log2(math.e)


def to_row(column):
    wide = jnp.broadcast_to(column, (column.shape[0], 128))
    copies = 128 // column.shape[0]
    return jnp.concatenate([wide] * copies, axis=0).T[0:1, :]


def to_column(row, count):
    return jnp.broadcast_to(row, (128, 128)).T[0:count, 0:1]


def join_log2(values):
    top = jnp.max(values, axis=0)
    return top + jnp.log2(jnp.sum(jnp.exp2(values - top[None]), axis=0))


def join_log(values):
    top = jnp.max(values, axis=0)
    return top + jnp.log(jnp.sum(jnp.exp(values - top[None]), axis=0))


def kernel(
    heads_axis, seq_axis, heads, queries_count,
    latent_q, turned_keys, query_ref, keys_ref, weight_ref,
    loss_out, query_out, prod_out, key_out,
    latent_keys, idx_q, flat_queries, weights, own_term, pair_recv, index_all, expo, base, stat_all, sum_send, sum_recv, act, dact, term, term_recv, loss_all,
    stat_send_sem, stat_recv_sem, sum_send_sem, sum_recv_sem,
    term_send_sem, term_recv_sem, loss_send_sem, loss_recv_sem, pair_send_sem, pair_recv_sem, index_send_sem, index_recv_sem,
):
    my_head = lax.axis_index("head")
    my_seq = lax.axis_index("seq")
    devices = heads_axis * seq_axis
    me = my_head * seq_axis + my_seq
    barrier = pltpu.get_barrier_semaphore()

    def place(index):
        return (index // seq_axis, lax.rem(index, seq_axis))

    def greet(offset, carry):
        other = lax.rem(me + offset, devices)
        pl.semaphore_signal(barrier, inc=1, device_id=place(other), device_id_type=MESH)
        return carry

    lax.fori_loop(1, devices, greet, 0)

    rows, width = latent_q.shape
    local_heads = rows // queries_count
    step = 256
    latent_keys[...] = turned_keys[...].T

    def attend(i, carry):
        columns = pl.ds(pl.multiple_of(i * step, step), step)
        scores = lax.dot_general(
            latent_keys[...], latent_q[columns, :], NT, preferred_element_type=F32
        )
        top = jnp.max(scores, axis=0, keepdims=True)
        part = jnp.exp2((scores - top) * exponent_scale)
        expo[:, columns] = part.astype(BF16)
        total = jnp.sum(part, axis=0, keepdims=True)
        base[:, columns] = top * exponent_scale
        stat_all[my_seq, :, columns] = top * exponent_scale + jnp.log2(total)
        return carry

    lax.fori_loop(0, rows // step, attend, 0)

    pl.semaphore_wait(barrier, devices - 1)

    def stat_copy(offset, source, target):
        return pltpu.make_async_remote_copy(
            src_ref=stat_all.at[source],
            dst_ref=stat_all.at[source],
            send_sem=stat_send_sem.at[offset],
            recv_sem=stat_recv_sem.at[source],
            device_id=(my_head, target),
            device_id_type=MESH,
        )

    def stat_start(offset, carry):
        stat_copy(offset, my_seq, lax.rem(my_seq + offset, seq_axis)).start()
        return carry

    def stat_wait(offset, carry):
        other = lax.rem(my_seq + offset, seq_axis)
        stat_copy(offset, other, other).wait_recv()
        return carry

    def stat_sent(offset, carry):
        stat_copy(offset, my_seq, lax.rem(my_seq + offset, seq_axis)).wait_send()
        return carry

    def index_copy(offset, source, target):
        return pltpu.make_async_remote_copy(
            src_ref=index_all.at[source],
            dst_ref=index_all.at[source],
            send_sem=index_send_sem.at[offset],
            recv_sem=index_recv_sem.at[source],
            device_id=(my_head, target),
            device_id_type=MESH,
        )

    def index_start(offset, carry):
        index_copy(offset, my_seq, lax.rem(my_seq + offset, seq_axis)).start()
        return carry

    def index_wait(offset, carry):
        other = lax.rem(my_seq + offset, seq_axis)
        index_copy(offset, other, other).wait_recv()
        return carry

    def index_sent(offset, carry):
        index_copy(offset, my_seq, lax.rem(my_seq + offset, seq_axis)).wait_send()
        return carry

    lax.fori_loop(1, seq_axis, stat_start, 0)

    blocks, block, _ = weights.shape
    fine = keys_ref.shape[0]
    group = math.gcd(blocks, 8)
    heads_in_block = block // queries_count
    wide = weight_ref[...].astype(F32)
    flat_queries[...] = query_ref[...].astype(F32)
    index_heads = wide.shape[1]
    for g in range(wide.shape[1]):
        row = g % heads_in_block * queries_count
        weights[g // heads_in_block, row : row + queries_count, :] = wide[:, g : g + 1]
        picked = flat_queries[pl.ds(g, queries_count, stride=index_heads), :]
        idx_q[g // heads_in_block, row : row + queries_count, :] = picked.astype(BF16)

    def index_scores(i, logits):
        queries = idx_q[pl.ds(i * group, group)]
        part = lax.dot_general(
            queries.reshape(group * block, -1), keys_ref[...], NT, preferred_element_type=F32
        )
        part = part.reshape(group, block, fine)
        act[pl.ds(i * group, group)] = part
        weighted = weights[pl.ds(i * group, group)] * jnp.maximum(part, 0.0)
        return logits + jnp.sum(
            weighted.reshape(group * heads_in_block, queries_count, fine), axis=0
        )

    logits = lax.fori_loop(
        0, blocks // group, index_scores, jnp.zeros((queries_count, fine), F32)
    )
    index_top = jnp.max(logits, axis=1, keepdims=True)
    index_total = jnp.sum(jnp.exp(logits - index_top), axis=1, keepdims=True)
    index_all[my_seq] = to_row(index_top + jnp.log(index_total))

    lax.fori_loop(1, seq_axis, index_start, 0)
    lax.fori_loop(1, seq_axis, stat_wait, 0)
    lax.fori_loop(1, seq_axis, index_wait, 0)

    joined = join_log2(stat_all[...])
    factor = jnp.exp2(base[...] - joined)
    upper = factor.astype(BF16).astype(F32)
    lower = factor - upper
    place_q = lax.broadcasted_iota(jnp.int32, (128, rows), 0)
    start = lax.broadcasted_iota(jnp.int32, (128, rows), 1)
    first = place_q * local_heads
    second = (place_q - queries_count) * local_heads
    in_first = jnp.logical_and(start >= first, start < first + local_heads)
    in_second = jnp.logical_and(start >= second, start < second + local_heads)
    spread = jnp.where(in_first, upper, jnp.where(in_second, lower, 0.0)).astype(BF16)
    summed = lax.dot_general(expo[...], spread, NT, preferred_element_type=F32).T
    summed = summed[0:queries_count] + summed[queries_count : 2 * queries_count]
    index_row = join_log(index_all[...])
    for j in range(heads_axis):
        sum_send[j, 0:queries_count, :] = summed[:, j * fine : (j + 1) * fine]
        sum_send[j, queries_count : queries_count + 1, 0:128] = index_row

    def sum_copy(offset, block_index, slot, target):
        return pltpu.make_async_remote_copy(
            src_ref=sum_send.at[block_index],
            dst_ref=sum_recv.at[slot],
            send_sem=sum_send_sem.at[offset],
            recv_sem=sum_recv_sem.at[slot],
            device_id=(target, my_seq),
            device_id_type=MESH,
        )

    for offset in range(1, heads_axis):
        target = lax.rem(my_head + offset, heads_axis)
        sum_copy(offset, target, my_head, target).start()
    targets = sum_send[my_head, 0:queries_count, :]
    index_rows = [index_row]
    for offset in range(1, heads_axis):
        source = lax.rem(my_head + offset, heads_axis)
        sum_copy(offset, source, source, source).wait_recv()
        targets = targets + sum_recv[source, 0:queries_count, :]
        index_rows.append(sum_recv[source, queries_count : queries_count + 1, 0:128])
    targets = targets / heads
    index_log = to_column(join_log(jnp.stack(index_rows)), queries_count)
    shifted = logits - index_log
    positive = targets > 0
    own_loss = jnp.where(positive, targets * jnp.log(jnp.where(positive, targets, 1.0)), 0.0)
    own_loss = jnp.sum(own_loss - targets * shifted, axis=0, keepdims=True)
    own_loss = sum(own_loss[:, i * 128 : (i + 1) * 128] for i in range(fine // 128))
    grad = jnp.exp(shifted) - targets
    loss_all[me] = own_loss

    def loss_copy(offset, slot, target):
        return pltpu.make_async_remote_copy(
            src_ref=loss_all.at[slot],
            dst_ref=loss_all.at[slot],
            send_sem=loss_send_sem.at[offset],
            recv_sem=loss_recv_sem.at[slot],
            device_id=place(target),
            device_id_type=MESH,
        )

    chunk = term.shape[1]
    owners = block // chunk

    def term_copy(source_slot, slot, target):
        return pltpu.make_async_remote_copy(
            src_ref=term.at[source_slot],
            dst_ref=term_recv.at[slot],
            send_sem=term_send_sem.at[source_slot],
            recv_sem=term_recv_sem.at[slot],
            device_id=place(target),
            device_id_type=MESH,
        )

    grads = jnp.concatenate([grad] * heads_in_block, axis=0)
    grad_upper = grads.astype(BF16).astype(F32)
    grad_lower = grads - grad_upper

    my_block = me // owners
    parity = lax.rem(my_seq, 2)
    pair = my_seq + 1 - 2 * parity

    def pair_copy(owner):
        return pltpu.make_async_remote_copy(
            src_ref=own_term.at[owner],
            dst_ref=pair_recv.at[owner],
            send_sem=pair_send_sem.at[owner],
            recv_sem=pair_recv_sem.at[owner],
            device_id=(my_head, pair),
            device_id_type=MESH,
        )

    def back(b):
        part = act[b]
        on = part > 0
        dact[b] = jnp.where(on, grads * weights[b], 0.0).astype(BF16)
        both = jnp.concatenate(
            [jnp.where(on, grad_upper, 0.0), jnp.where(on, grad_lower, 0.0)], axis=0
        ).astype(BF16)
        result = jnp.dot(both, keys_ref[...], preferred_element_type=F32)
        result = result[0:block] + result[block : 2 * block]
        for j in range(owners):
            own_term[b * owners + j] = result[j * chunk : (j + 1) * chunk]

    def finish(owner):
        pair_copy(owner).wait_recv()
        term[owner] = (own_term[owner] + pair_recv[owner]).astype(BF16)

        @pl.when(owner != me)
        def _():
            term_copy(owner, me, owner).start()

    half = devices // 2

    def partner_owner(offset):
        return lax.rem(2 * (me // 2 + offset), devices) + 1 - parity

    def kept_owner(offset):
        return lax.rem(2 * (me // 2 + offset), devices) + parity

    if owners == 1:

        def first_half(offset, carry):
            back(partner_owner(offset))
            pair_copy(partner_owner(offset)).start()
            return carry

        def second_half(offset, carry):
            back(kept_owner(offset))
            finish(kept_owner(offset))
            return carry

        lax.fori_loop(1, half + 1, first_half, 0)
        lax.fori_loop(1, half + 1, second_half, 0)
    else:

        def every_block(b, carry):
            back(b)
            return carry

        def pair_start(offset, carry):
            pair_copy(partner_owner(offset)).start()
            return carry

        def finish_all(offset, carry):
            finish(kept_owner(offset))
            return carry

        lax.fori_loop(0, blocks, every_block, 0)
        lax.fori_loop(1, half + 1, pair_start, 0)
        lax.fori_loop(1, half + 1, finish_all, 0)

    def loss_start(offset, carry):
        loss_copy(offset, me, lax.rem(me + offset, devices)).start()
        return carry

    lax.fori_loop(1, devices, loss_start, 0)

    key_out[...] = lax.dot_general(
        dact[...].reshape(blocks * block, fine),
        idx_q[...].reshape(blocks * block, -1),
        TN,
        preferred_element_type=F32,
    )

    def term_wait(offset, total):
        source = kept_owner(offset)
        term_copy(source, source, source).wait_recv()
        return total + term_recv[source].astype(F32)

    total = lax.fori_loop(1, half, term_wait, own_term[me] + pair_recv[me])
    own_block = my_block
    inner = me - my_block * owners
    own_weights = weights[own_block]
    own_queries = idx_q[own_block].astype(F32)
    if owners == 1:
        query_out[...] = total * own_weights
        prod_out[...] = total * own_queries
    else:
        for j in range(owners):

            @pl.when(inner == j)
            def _():
                query_out[...] = total * own_weights[j * chunk : (j + 1) * chunk]
                prod_out[...] = total * own_queries[j * chunk : (j + 1) * chunk]

    def loss_wait(offset, carry):
        source = lax.rem(me + offset, devices)
        loss_copy(offset, source, source).wait_recv()
        return carry

    lax.fori_loop(1, devices, loss_wait, 0)
    loss_out[...] = jnp.sum(loss_all[...], axis=0)

    lax.fori_loop(1, seq_axis, stat_sent, 0)
    lax.fori_loop(1, seq_axis, index_sent, 0)
    for offset in range(1, heads_axis):
        target = lax.rem(my_head + offset, heads_axis)
        sum_copy(offset, target, my_head, target).wait_send()

    def last_sent(offset, carry):
        other = lax.rem(me + offset, devices)
        loss_copy(offset, me, other).wait_send()
        return carry

    def half_sent(offset, carry):
        term_copy(kept_owner(offset), me, kept_owner(offset)).wait_send()
        return carry

    def pair_sent(offset, carry):
        pair_copy(partner_owner(offset)).wait_send()
        return carry

    lax.fori_loop(1, devices, last_sent, 0)
    lax.fori_loop(1, half, half_sent, 0)
    lax.fori_loop(1, half + 1, pair_sent, 0)


def closing(queries_count, loss_in, query_in, prod_in, key_in, loss_out, query_out, weight_out, key_out):
    loss_out[...] = jnp.sum(loss_in[...], axis=1, keepdims=True) / queries_count
    query_out[...] = query_in[...]
    ones = jnp.ones((8, prod_in.shape[1]), F32)
    sums = lax.dot_general(
        ones, prod_in[...], NT, precision=lax.Precision.HIGHEST, preferred_element_type=F32
    )
    weight_out[...] = sums[0:1]
    key_out[...] = key_in[...]


def shards(heads_axis, seq_axis, latent_q, latent_keys, idx_q, idx_keys, idx_weight):
    queries_count, local_heads, width = latent_q.shape
    index_heads, size = idx_q.shape[1:]
    rows = queries_count * local_heads
    keys = latent_keys.shape[0]
    fine = idx_keys.shape[1]
    devices = heads_axis * seq_axis
    all_rows = queries_count * index_heads
    chunk = all_rows // devices
    block = max(chunk, queries_count)
    blocks = all_rows // block
    queries = idx_q.reshape(all_rows, size)
    vmem = pl.BlockSpec(memory_space=pltpu.VMEM)
    dma = pltpu.SemaphoreType.DMA
    loss, query_grad, prod, key_grad = pl.pallas_call(
        functools.partial(
            kernel, heads_axis, seq_axis, local_heads * heads_axis, queries_count
        ),
        out_shape=(
            jax.ShapeDtypeStruct((1, 128), F32),
            jax.ShapeDtypeStruct((chunk, size), F32),
            jax.ShapeDtypeStruct((chunk, size), F32),
            jax.ShapeDtypeStruct((fine, size), F32),
        ),
        in_specs=[vmem] * 5,
        out_specs=(vmem,) * 4,
        scratch_shapes=[
            pltpu.VMEM((keys, width), BF16),
            pltpu.VMEM((blocks, block, size), BF16),
            pltpu.VMEM((all_rows, size), F32),
            pltpu.VMEM((blocks, block, 1), F32),
            pltpu.VMEM((devices, chunk, size), F32),
            pltpu.VMEM((devices, chunk, size), F32),
            pltpu.VMEM((seq_axis, 1, 128), F32),
            pltpu.VMEM((keys, rows), BF16),
            pltpu.VMEM((1, rows), F32),
            pltpu.VMEM((seq_axis, 1, rows), F32),
            pltpu.VMEM((heads_axis, queries_count + 8, fine), F32),
            pltpu.VMEM((heads_axis, queries_count + 8, fine), F32),
            pltpu.VMEM((blocks, block, fine), F32),
            pltpu.VMEM((blocks, block, fine), BF16),
            pltpu.VMEM((devices, chunk, size), BF16),
            pltpu.VMEM((devices, chunk, size), BF16),
            pltpu.VMEM((devices, 1, 128), F32),
            dma((seq_axis,)),
            dma((seq_axis,)),
            dma((heads_axis,)),
            dma((heads_axis,)),
            dma((devices,)),
            dma((devices,)),
            dma((devices,)),
            dma((devices,)),
            dma((devices,)),
            dma((devices,)),
            dma((seq_axis,)),
            dma((seq_axis,)),
        ],
        compiler_params=pltpu.CompilerParams(
            collective_id=0, has_side_effects=True, vmem_limit_bytes=60 * 1024 * 1024
        ),
    )(latent_q.reshape(rows, width), latent_keys.T, queries, idx_keys[0], idx_weight)
    loss, query_grad, weight_grad, key_grad = pl.pallas_call(
        functools.partial(closing, queries_count),
        out_shape=(
            jax.ShapeDtypeStruct((1, 1), F32),
            jax.ShapeDtypeStruct((chunk, size), F32),
            jax.ShapeDtypeStruct((1, chunk), F32),
            jax.ShapeDtypeStruct((fine, size), F32),
        ),
        in_specs=[vmem] * 4,
        out_specs=(vmem,) * 4,
    )(loss, query_grad, prod, key_grad)
    return (loss.reshape(()), query_grad, weight_grad.reshape(-1), key_grad[None])


def solution(mesh):
    in_specs = (P(None, "head", None), P("seq", None), P(), P("seq", "head", None), P())
    out_specs = (P(), P(("head", "seq"), None), P(("head", "seq")), P("seq", "head", None))
    body = functools.partial(shards, mesh.shape["head"], mesh.shape["seq"])
    return jax.shard_map(body, mesh=mesh, in_specs=in_specs, out_specs=out_specs, check_vma=False)
```
